32 devices in a mesh: dp: 4 (over y, x), mp: 8 (over z, core).
Axes of the slice: x: 2, y: 2, z: 4, core: 2. Of those that a mesh axis runs over, the one named last changes fastest.
Arguments:
- tokens: bfloat16 [1024, 8192], P('dp', 'mp'), may hold values from -6 to 6
- base_weight: bfloat16 [24576, 8192], P('mp'), may hold values from -0.0625 to 0.0625
- block_values: bfloat16 [256, 128, 128], P('mp'), may hold values from -0.0625 to 0.0625
- block_ids: int32 [2, 256], P(None, 'mp'), may hold values from -1 to 63, as said below
- lowrank_model: float32 [8192, 256], P('mp'), may hold values from -6 to 6
- lowrank_hidden: float32 [24576, 256], P('mp'), may hold values from -6 to 6
- output_cotangent: bfloat16 [1024, 24576], P('dp', 'mp'), may hold values from -6 to 6
Outputs:
- projection_output: bfloat16 [1024, 24576], P('dp', 'mp')
- input_cotangent: bfloat16 [1024, 8192], P('dp', 'mp')
- block_grads: float32 [256, 128, 128], P(('mp', 'dp'))
- updated_model: float32 [8192, 256], P('mp')
- updated_hidden: float32 [24576, 256], P('mp')
The draws below stay inside these ranges and needn't reach their ends.
Inputs may be any that keep to these rules, and one draw needn't show every extreme that they name: `block_ids`: slots 32 * m to 32 * (m + 1) - 1 belong to index m of mp. A live slot has row 0 in 0 to 23 and row 1 in 0 to 63; the live slots of one index come first and name distinct blocks; the remaining slots hold -1 in both rows. Every index has 8 or more live slots, and some index has all 32.
All inputs are finite; a program needn't handle non-finite values.
Results may differ from the reference program's by a relative error of at most 0.0065.
Values may be sent and summed in bfloat16 or wider, within the bound.
A program may use at most 384 MiB of HBM per device.

```python
import math
import jax
import jax.numpy as jnp
from jax import lax

MODEL_WIDTH = 8192
F = 24576
BLK = 128
ADAPTER_RANK = 256
NB_DEV = 32
TOKENS = 1024
FB_DEV = 24
DB = 64
NB = 256
N_MP = 8


def draw_block_ids(key, part):
    device_count = NB // NB_DEV
    base_key = jax.random.fold_in(key, 11)
    device_keys = jax.random.split(base_key, device_count)

    def pick_one(one_key):
        order_key, count_key = jax.random.split(one_key)
        picks = jax.random.permutation(order_key, FB_DEV * DB)[:NB_DEV].astype(jnp.int32)
        counts = jax.random.randint(count_key, (), NB_DEV // 4, NB_DEV + 1, dtype=jnp.int32)
        return (picks, counts)
    picks, counts = jax.vmap(pick_one)(device_keys)
    fullest = jax.random.randint(jax.random.fold_in(key, 12), (), 0, device_count, dtype=jnp.int32)
    counts = jnp.where(jnp.arange(device_count, dtype=jnp.int32) == fullest, NB_DEV, counts)
    slot_index = jnp.arange(NB_DEV, dtype=jnp.int32)
    live_slots = slot_index[None, :] < counts[:, None]
    row_part = jnp.where(live_slots, picks // DB, -1).reshape(-1)
    col_part = jnp.where(live_slots, picks % DB, -1).reshape(-1)
    return jnp.stack([row_part, col_part]).astype(jnp.int32)


def draw_output_cotangent(key, part):
    base_key = jax.random.fold_in(key, 21)
    values = jax.random.normal(base_key, (TOKENS, F), jnp.float32)
    strength = 0.2
    for term_index in range(8):
        sign_key = jax.random.fold_in(key, 100 + term_index)
        row_key = jax.random.fold_in(key, 200 + term_index)
        signs = jax.random.rademacher(sign_key, (TOKENS,), dtype=jnp.float32)
        hidden_row = jax.random.normal(row_key, (F,), jnp.float32)
        values = values + strength * signs[:, None] * hidden_row[None, :]
    return jnp.clip(values, -6.0, 6.0).astype(jnp.bfloat16)


def steps_of(key, shape, cuts, smallest, top_value):
    factor_of, own = 1.0, jax.random.fold_in(key, 6)
    for axis_at, shards_of in cuts:
        heights = jnp.exp(jax.random.uniform(jax.random.fold_in(own, axis_at), (shards_of,), jnp.float32, smallest / len(cuts), top_value / len(cuts)))
        factor_of = factor_of * jnp.repeat(heights, shape[axis_at] // shards_of).reshape([-1 if axis == axis_at else 1 for axis in range(len(shape))])
    return factor_of


def bell_draw(stream_key, dims, width, most, cuts=(), kind=jnp.bfloat16):
    drawn = width * jax.random.normal(stream_key, dims, jnp.float32)
    if cuts:
        drawn = drawn * steps_of(stream_key, dims, cuts, -0.22, 0.18)
    return jnp.clip(drawn, -most, most).astype(kind)


def setup_inputs(seed: int = 0) -> dict:
    key_of = jax.random.split(jax.random.key(seed), 8)
    tokens = bell_draw(key_of[0], (TOKENS, MODEL_WIDTH), 1.0, 6.0, ((0, 4), (1, 8)))
    base_weight = bell_draw(key_of[1], (F, MODEL_WIDTH), MODEL_WIDTH ** -0.5, 0.0625, ((0, 8),))
    block_values = bell_draw(key_of[2], (NB, BLK, BLK), MODEL_WIDTH ** -0.5, 0.0625, ((0, 8),))
    block_ids = draw_block_ids(jax.random.fold_in(key_of[7], 71), 0)
    lowrank_model = bell_draw(key_of[4], (MODEL_WIDTH, ADAPTER_RANK), 1.0, 6.0, ((0, 8),), jnp.float32)
    lowrank_hidden = bell_draw(key_of[5], (F, ADAPTER_RANK), 1.0, 6.0, ((0, 8),), jnp.float32)
    output_cotangent = draw_output_cotangent(jax.random.fold_in(key_of[7], 71), 0)
    return dict(tokens=tokens, base_weight=base_weight, block_values=block_values, block_ids=block_ids, lowrank_model=lowrank_model, lowrank_hidden=lowrank_hidden, output_cotangent=output_cotangent)


def build_sparse(block_values, block_ids):
    slot_index = jnp.arange(NB, dtype=jnp.int32)
    device_index = slot_index // NB_DEV
    row_ids = block_ids[0]
    col_ids = block_ids[1]
    live_slots = row_ids >= 0
    global_rows = device_index * FB_DEV + row_ids
    flat_index = jnp.where(live_slots, global_rows * DB + col_ids, F // BLK * DB).astype(jnp.int32)
    sparse = jnp.zeros((F // BLK * DB, BLK, BLK), jnp.bfloat16)
    sparse = sparse.at[flat_index].add(block_values, mode='drop')
    sparse = sparse.reshape(F // BLK, DB, BLK, BLK).transpose(0, 2, 1, 3).reshape(F, MODEL_WIDTH)
    return sparse

def block_gradients(tokens, output_cotangent, block_ids):
    grad_blocks3 = output_cotangent.reshape(TOKENS, F // BLK, BLK)
    token_blocks3 = tokens.reshape(TOKENS, DB, BLK)

    def one_device(device_index):
        ids_here = lax.dynamic_slice(block_ids, (jnp.int32(0), (device_index * NB_DEV).astype(jnp.int32)), (2, NB_DEV))
        live_slots = ids_here[0] >= 0
        safe_rows = device_index * FB_DEV + jnp.maximum(ids_here[0], 0)
        safe_cols = jnp.maximum(ids_here[1], 0)
        grad_sel = jnp.take(grad_blocks3, safe_rows, axis=1).astype(jnp.float32)
        token_sel = jnp.take(token_blocks3, safe_cols, axis=1).astype(jnp.float32)
        summed = jnp.einsum('tbi,tbj->bij', grad_sel, token_sel)
        return summed * live_slots.astype(jnp.float32)[:, None, None] / math.sqrt(TOKENS)
    per_device = lax.map(one_device, jnp.arange(N_MP, dtype=jnp.int32))
    return per_device.reshape(NB, BLK, BLK)

def reference(tokens, base_weight, block_values, block_ids, lowrank_model, lowrank_hidden, output_cotangent):
    sparse = build_sparse(block_values, block_ids)
    effective = (base_weight.astype(jnp.float32) + sparse.astype(jnp.float32)).astype(jnp.bfloat16)
    adapter_scale = 0.5 / math.sqrt(ADAPTER_RANK * MODEL_WIDTH)
    model_half = lowrank_model.astype(jnp.bfloat16)
    hidden_half = lowrank_hidden.astype(jnp.bfloat16)
    left_factor_shard = jnp.dot(tokens.astype(jnp.float32), model_half.astype(jnp.float32), preferred_element_type=jnp.float32).astype(jnp.bfloat16)
    right_factor_shard = jnp.dot(output_cotangent.astype(jnp.float32), hidden_half.astype(jnp.float32), preferred_element_type=jnp.float32).astype(jnp.bfloat16)
    base_projection_output = lax.dot_general(tokens.astype(jnp.float32), effective.astype(jnp.float32), (((1,), (1,)), ((), ())), preferred_element_type=jnp.float32)
    lowrank_output = lax.dot_general(left_factor_shard.astype(jnp.float32), hidden_half.astype(jnp.float32), (((1,), (1,)), ((), ())), preferred_element_type=jnp.float32)
    projection_output = (base_projection_output + adapter_scale * lowrank_output).astype(jnp.bfloat16)
    backward_base_term = jnp.dot(output_cotangent.astype(jnp.float32), effective.astype(jnp.float32), preferred_element_type=jnp.float32)
    backward_lowrank_term = lax.dot_general(right_factor_shard.astype(jnp.float32), model_half.astype(jnp.float32), (((1,), (1,)), ((), ())), preferred_element_type=jnp.float32)
    input_cotangent = (backward_base_term + adapter_scale * backward_lowrank_term).astype(jnp.bfloat16)
    block_grads = block_gradients(tokens, output_cotangent, block_ids)
    hidden_side_gradient = adapter_scale * lax.dot_general(output_cotangent.astype(jnp.float32), left_factor_shard.astype(jnp.float32), (((0,), (0,)), ((), ())), preferred_element_type=jnp.float32)
    model_side_gradient = adapter_scale * lax.dot_general(tokens.astype(jnp.float32), right_factor_shard.astype(jnp.float32), (((0,), (0,)), ((), ())), preferred_element_type=jnp.float32)
    model_step = lowrank_model - math.sqrt(ADAPTER_RANK * MODEL_WIDTH / (TOKENS * F)) * model_side_gradient
    moved = lowrank_hidden - math.sqrt(ADAPTER_RANK / TOKENS) * hidden_side_gradient
    gram = lax.dot_general(moved, moved, (((0,), (0,)), ((), ())), precision=lax.Precision.HIGHEST)
    lower = jnp.linalg.cholesky(gram)
    solved = lax.linalg.triangular_solve(lower, moved, left_side=False, lower=True, transpose_a=True)
    updated_hidden = math.sqrt(F) * solved
    updated_model = jnp.dot(model_step, lower, precision=lax.Precision.HIGHEST) / math.sqrt(F)
    return (projection_output, input_cotangent, block_grads, updated_model, updated_hidden)
```

```python
import functools
import math

import jax
import jax.numpy as jnp
from jax import lax
from jax.experimental import pallas as pl
from jax.experimental.pallas import tpu as pltpu
from jax.sharding import PartitionSpec as P

HIGHEST = lax.Precision.HIGHEST


def largest_divisor(total, step, most):
    return max(c for c in range(step, most + 1, step) if total % c == 0)


def dense_kernel(
    lora_scale,
    grad_scale,
    tile,
    chunk,
    ids_ref,
    tok_ref,
    cot_ref,
    hid_ref,
    u_ref,
    vals_ref,
    base_ref,
    out_ref,
    back_ref,
    grads_ref,
    buf,
    acc_out,
    acc_back,
    sem,
):
    hidden, width = base_ref.shape
    slots, side = vals_ref.shape[0], vals_ref.shape[1]
    parts, _, part_width = back_ref.shape
    tiles = hidden // tile
    per_tile = tile // side

    def fetch(step, slot):
        rows = pl.ds(pl.multiple_of(step * tile, tile), tile)
        return pltpu.make_async_copy(base_ref.at[rows], buf.at[slot], sem.at[slot])

    fetch(0, 0).start()
    grads_ref[...] = jnp.zeros_like(grads_ref)

    @pl.loop(0, tiles)
    def _(step):
        slot = lax.rem(step, 2)

        @pl.when(step + 1 < tiles)
        def _():
            fetch(step + 1, 1 - slot).start()

        fetch(step, slot).wait()

        @pl.loop(0, slots)
        def _(s):
            row = ids_ref[0, s]

            @pl.when((row >= step * per_tile) & (row < (step + 1) * per_tile))
            def _():
                cols = pl.ds(pl.multiple_of(ids_ref[1, s] * side, side), side)
                inner = pl.ds(pl.multiple_of((row - step * per_tile) * side, side), side)
                outer = pl.ds(pl.multiple_of(row * side, side), side)
                old = buf[slot, inner, cols].astype(jnp.float32)
                buf[slot, inner, cols] = (old + vals_ref[s].astype(jnp.float32)).astype(buf.dtype)
                block = lax.dot_general(
                    cot_ref[:, outer],
                    tok_ref[:, cols],
                    (((0,), (0,)), ((), ())),
                    preferred_element_type=jnp.float32,
                )
                grads_ref[s] = (block * grad_scale).astype(grads_ref.dtype)

        rows = pl.ds(pl.multiple_of(step * tile, tile), tile)
        acc_out[...] = lora_scale * lax.dot_general(
            u_ref[...],
            hid_ref[rows, :],
            (((1,), (1,)), ((), ())),
            preferred_element_type=jnp.float32,
        )

        @pl.loop(0, width // chunk)
        def _(c):
            cols = pl.ds(pl.multiple_of(c * chunk, chunk), chunk)
            weights = buf[slot, :, cols]
            acc_out[...] += lax.dot_general(
                tok_ref[:, cols],
                weights,
                (((1,), (1,)), ((), ())),
                preferred_element_type=jnp.float32,
            )
            term = jnp.dot(cot_ref[:, rows], weights, preferred_element_type=jnp.float32)

            @pl.when(step == 0)
            def _():
                acc_back[:, cols] = term

            @pl.when(step > 0)
            def _():
                acc_back[:, cols] += term

        out_ref[:, rows] = acc_out[...].astype(out_ref.dtype)

    for part in range(parts):
        back_ref[part] = acc_back[:, part * part_width : (part + 1) * part_width].astype(
            back_ref.dtype
        )


def dense(ids, gathered, cotangent, hidden_half, u_half, values, base, parts, lora_scale, grad_scale):
    rows, width = gathered.shape
    hidden = base.shape[0]
    tile = largest_divisor(hidden, values.shape[1], 512)
    chunk = largest_divisor(width, values.shape[1], 1024)
    vmem = pl.BlockSpec(memory_space=pltpu.VMEM)
    return pl.pallas_call(
        functools.partial(dense_kernel, lora_scale, grad_scale, tile, chunk),
        out_shape=(
            jax.ShapeDtypeStruct((rows, hidden), jnp.bfloat16),
            jax.ShapeDtypeStruct((parts, rows, width // parts), jnp.bfloat16),
            jax.ShapeDtypeStruct(values.shape, jnp.bfloat16),
        ),
        in_specs=[pl.BlockSpec(memory_space=pltpu.SMEM)]
        + [vmem] * 5
        + [pl.BlockSpec(memory_space=pl.ANY)],
        out_specs=(vmem, vmem, vmem),
        scratch_shapes=[
            pltpu.VMEM((2, tile, width), jnp.bfloat16),
            pltpu.VMEM((rows, tile), jnp.float32),
            pltpu.VMEM((rows, width), jnp.float32),
            pltpu.SemaphoreType.DMA((2,)),
        ],
        compiler_params=pltpu.CompilerParams(vmem_limit_bytes=60 * 1024 * 1024),
        cost_estimate=pl.CostEstimate(
            flops=4 * rows * hidden * width,
            bytes_accessed=2 * hidden * width + 4 * rows * width,
            transcendentals=0,
        ),
    )(ids, gathered, cotangent, hidden_half, u_half, values, base)


def shards(
    tokens, base_weight, block_values, block_ids, lowrank_model, lowrank_hidden, output_cotangent
):
    mp_size = lax.axis_size("mp")
    total_tokens = tokens.shape[0] * lax.axis_size("dp")
    feature_width = base_weight.shape[1]
    hidden_total = base_weight.shape[0] * mp_size
    rank = lowrank_model.shape[1]
    lora_scale = 0.5 / math.sqrt(rank * feature_width)

    model_half = lowrank_model.astype(jnp.bfloat16)
    hidden_half = lowrank_hidden.astype(jnp.bfloat16)
    gathered = lax.all_gather(tokens, "mp", axis=1, tiled=True)
    u_part = jnp.dot(tokens, model_half, preferred_element_type=jnp.float32)
    v_part = jnp.dot(output_cotangent, hidden_half, preferred_element_type=jnp.float32)
    both = lax.psum(jnp.stack([u_part, v_part]), "mp").astype(jnp.bfloat16)
    u_half, v_half = both[0], both[1]

    hidden_part = lora_scale * lax.dot_general(
        output_cotangent, u_half, (((0,), (0,)), ((), ())), preferred_element_type=jnp.float32
    )
    model_part = lora_scale * lax.dot_general(
        tokens, v_half, (((0,), (0,)), ((), ())), preferred_element_type=jnp.float32
    )
    grad_hidden, grad_model = lax.psum(
        (hidden_part.astype(jnp.bfloat16), model_part.astype(jnp.bfloat16)), "dp"
    )

    projection_output, back_parts, block_parts = dense(
        block_ids,
        gathered,
        output_cotangent,
        hidden_half,
        u_half,
        block_values,
        base_weight,
        mp_size,
        lora_scale,
        1.0 / math.sqrt(total_tokens),
    )

    model_step = lowrank_model - math.sqrt(
        rank * feature_width / (total_tokens * hidden_total)
    ) * grad_model.astype(jnp.float32)
    moved = lowrank_hidden - math.sqrt(rank / total_tokens) * grad_hidden.astype(jnp.float32)
    gram = lax.psum(
        lax.dot_general(moved, moved, (((0,), (0,)), ((), ())), precision=HIGHEST), "mp"
    )
    lower = lax.linalg.cholesky(gram, symmetrize_input=False)
    inverse = lax.linalg.triangular_solve(
        lower, math.sqrt(hidden_total) * jnp.eye(rank, dtype=jnp.float32), left_side=True, lower=True
    )
    updated_hidden = lax.dot_general(
        moved, inverse, (((1,), (1,)), ((), ())), precision=HIGHEST
    )
    updated_model = jnp.dot(model_step, lower, precision=HIGHEST) / math.sqrt(hidden_total)

    back = lax.psum_scatter(back_parts, "mp", scatter_dimension=0, tiled=False)
    lowrank_back = lax.dot_general(
        v_half, model_half, (((1,), (1,)), ((), ())), preferred_element_type=jnp.float32
    )
    input_cotangent = (back.astype(jnp.float32) + lora_scale * lowrank_back).astype(jnp.bfloat16)
    block_grads = lax.psum_scatter(block_parts, "dp", scatter_dimension=0, tiled=True).astype(
        jnp.float32
    )
    return (projection_output, input_cotangent, block_grads, updated_model, updated_hidden)


def solution(mesh):
    in_specs = (
        P("dp", "mp"),
        P("mp", None),
        P("mp", None, None),
        P(None, "mp"),
        P("mp", None),
        P("mp", None),
        P("dp", "mp"),
    )
    out_specs = (
        P("dp", "mp"),
        P("dp", "mp"),
        P(("mp", "dp"), None, None),
        P("mp", None),
        P("mp", None),
    )
    return jax.shard_map(shards, mesh=mesh, in_specs=in_specs, out_specs=out_specs, check_vma=False)
```

```python
import functools
import math

import jax
import jax.numpy as jnp
from jax import lax
from jax.experimental import pallas as pl
from jax.experimental.pallas import tpu as pltpu
from jax.sharding import PartitionSpec as P

HIGHEST = lax.Precision.HIGHEST


def largest_divisor(total, step, most):
    return max(c for c in range(step, most + 1, step) if total % c == 0)


def dense_kernel(
    lora_scale,
    grad_scale,
    tile,
    chunk,
    ids_ref,
    tok_ref,
    cot_ref,
    hid_ref,
    u_ref,
    vals_ref,
    base_ref,
    out_ref,
    back_ref,
    grads_ref,
    buf,
    acc_out,
    acc_back,
    sem,
):
    hidden, width = base_ref.shape
    slots, side = vals_ref.shape[0], vals_ref.shape[1]
    parts, _, part_width = back_ref.shape
    tiles = hidden // tile
    per_tile = tile // side

    def fetch(step, slot):
        rows = pl.ds(pl.multiple_of(step * tile, tile), tile)
        return pltpu.make_async_copy(base_ref.at[rows], buf.at[slot], sem.at[slot])

    fetch(0, 0).start()
    grads_ref[...] = jnp.zeros_like(grads_ref)

    @pl.loop(0, tiles)
    def _(step):
        slot = lax.rem(step, 2)

        @pl.when(step + 1 < tiles)
        def _():
            fetch(step + 1, 1 - slot).start()

        fetch(step, slot).wait()

        @pl.loop(0, slots)
        def _(s):
            row = ids_ref[0, s]

            @pl.when((row >= step * per_tile) & (row < (step + 1) * per_tile))
            def _():
                cols = pl.ds(pl.multiple_of(ids_ref[1, s] * side, side), side)
                inner = pl.ds(pl.multiple_of((row - step * per_tile) * side, side), side)
                outer = pl.ds(pl.multiple_of(row * side, side), side)
                old = buf[slot, inner, cols].astype(jnp.float32)
                buf[slot, inner, cols] = (old + vals_ref[s].astype(jnp.float32)).astype(buf.dtype)
                block = lax.dot_general(
                    cot_ref[:, outer],
                    tok_ref[:, cols],
                    (((0,), (0,)), ((), ())),
                    preferred_element_type=jnp.float32,
                )
                grads_ref[s] = (block * grad_scale).astype(grads_ref.dtype)

        rows = pl.ds(pl.multiple_of(step * tile, tile), tile)
        acc_out[...] = lora_scale * lax.dot_general(
            u_ref[...],
            hid_ref[rows, :],
            (((1,), (1,)), ((), ())),
            preferred_element_type=jnp.float32,
        )

        @pl.loop(0, width // chunk)
        def _(c):
            cols = pl.ds(pl.multiple_of(c * chunk, chunk), chunk)
            weights = buf[slot, :, cols]
            acc_out[...] += lax.dot_general(
                tok_ref[:, cols],
                weights,
                (((1,), (1,)), ((), ())),
                preferred_element_type=jnp.float32,
            )
            term = jnp.dot(cot_ref[:, rows], weights, preferred_element_type=jnp.float32)

            @pl.when(step == 0)
            def _():
                acc_back[:, cols] = term

            @pl.when(step > 0)
            def _():
                acc_back[:, cols] += term

        out_ref[:, rows] = acc_out[...].astype(out_ref.dtype)

    for part in range(parts):
        back_ref[part] = acc_back[:, part * part_width : (part + 1) * part_width].astype(
            back_ref.dtype
        )


def dense(ids, gathered, cotangent, hidden_half, u_half, values, base, parts, lora_scale, grad_scale):
    rows, width = gathered.shape
    hidden = base.shape[0]
    tile = largest_divisor(hidden, values.shape[1], 512)
    chunk = largest_divisor(width, values.shape[1], 1024)
    vmem = pl.BlockSpec(memory_space=pltpu.VMEM)
    return pl.pallas_call(
        functools.partial(dense_kernel, lora_scale, grad_scale, tile, chunk),
        out_shape=(
            jax.ShapeDtypeStruct((rows, hidden), jnp.bfloat16),
            jax.ShapeDtypeStruct((parts, rows, width // parts), jnp.bfloat16),
            jax.ShapeDtypeStruct(values.shape, jnp.bfloat16),
        ),
        in_specs=[pl.BlockSpec(memory_space=pltpu.SMEM)]
        + [vmem] * 5
        + [pl.BlockSpec(memory_space=pl.ANY)],
        out_specs=(vmem, vmem, vmem),
        scratch_shapes=[
            pltpu.VMEM((2, tile, width), jnp.bfloat16),
            pltpu.VMEM((rows, tile), jnp.float32),
            pltpu.VMEM((rows, width), jnp.float32),
            pltpu.SemaphoreType.DMA((2,)),
        ],
        compiler_params=pltpu.CompilerParams(vmem_limit_bytes=60 * 1024 * 1024),
        cost_estimate=pl.CostEstimate(
            flops=4 * rows * hidden * width,
            bytes_accessed=2 * hidden * width + 4 * rows * width,
            transcendentals=0,
        ),
    )(ids, gathered, cotangent, hidden_half, u_half, values, base)


def factor_and_inverse(gram):
    half = gram.shape[0] // 2
    eye = jnp.eye(half, dtype=gram.dtype)
    zero = jnp.zeros((half, half), gram.dtype)

    def corner(block):
        low = lax.linalg.cholesky(block, symmetrize_input=False)
        return low, lax.linalg.triangular_solve(low, eye, left_side=True, lower=True)

    low1, inv1 = corner(gram[:half, :half])
    cross = lax.dot_general(
        gram[half:, :half], inv1, (((1,), (1,)), ((), ())), precision=HIGHEST
    )
    square = lax.dot_general(cross, cross, (((1,), (1,)), ((), ())), precision=HIGHEST)
    low2, inv2 = corner(gram[half:, half:] - square)
    below = -jnp.dot(inv2, jnp.dot(cross, inv1, precision=HIGHEST), precision=HIGHEST)
    lower = jnp.block([[low1, zero], [cross, low2]])
    inverse = jnp.block([[inv1, zero], [below, inv2]])
    return lower, inverse


def shards(
    tokens, base_weight, block_values, block_ids, lowrank_model, lowrank_hidden, output_cotangent
):
    mp_size = lax.axis_size("mp")
    total_tokens = tokens.shape[0] * lax.axis_size("dp")
    feature_width = base_weight.shape[1]
    hidden_total = base_weight.shape[0] * mp_size
    rank = lowrank_model.shape[1]
    lora_scale = 0.5 / math.sqrt(rank * feature_width)

    model_half = lowrank_model.astype(jnp.bfloat16)
    hidden_half = lowrank_hidden.astype(jnp.bfloat16)
    gathered = lax.all_gather(tokens, "mp", axis=1, tiled=True)
    u_part = jnp.dot(tokens, model_half, preferred_element_type=jnp.float32)
    v_part = jnp.dot(output_cotangent, hidden_half, preferred_element_type=jnp.float32)
    both = lax.psum(jnp.stack([u_part, v_part]), "mp").astype(jnp.bfloat16)
    u_half, v_half = both[0], both[1]

    hidden_part = lora_scale * lax.dot_general(
        output_cotangent, u_half, (((0,), (0,)), ((), ())), preferred_element_type=jnp.float32
    )
    model_part = lora_scale * lax.dot_general(
        tokens, v_half, (((0,), (0,)), ((), ())), preferred_element_type=jnp.float32
    )
    grad_hidden, grad_model = lax.psum(
        (hidden_part.astype(jnp.bfloat16), model_part.astype(jnp.bfloat16)), "dp"
    )

    projection_output, back_parts, block_parts = dense(
        block_ids,
        gathered,
        output_cotangent,
        hidden_half,
        u_half,
        block_values,
        base_weight,
        mp_size,
        lora_scale,
        1.0 / math.sqrt(total_tokens),
    )

    model_step = lowrank_model - math.sqrt(
        rank * feature_width / (total_tokens * hidden_total)
    ) * grad_model.astype(jnp.float32)
    moved = lowrank_hidden - math.sqrt(rank / total_tokens) * grad_hidden.astype(jnp.float32)
    gram = lax.psum(
        lax.dot_general(moved, moved, (((0,), (0,)), ((), ())), precision=HIGHEST), "mp"
    )
    lower, inverse = factor_and_inverse(gram)
    inverse = math.sqrt(hidden_total) * inverse
    updated_hidden = lax.dot_general(
        moved, inverse, (((1,), (1,)), ((), ())), precision=HIGHEST
    )
    updated_model = jnp.dot(model_step, lower, precision=HIGHEST) / math.sqrt(hidden_total)

    back = lax.psum_scatter(back_parts, "mp", scatter_dimension=0, tiled=False)
    lowrank_back = lax.dot_general(
        v_half, model_half, (((1,), (1,)), ((), ())), preferred_element_type=jnp.float32
    )
    input_cotangent = (back.astype(jnp.float32) + lora_scale * lowrank_back).astype(jnp.bfloat16)
    block_grads = lax.psum_scatter(block_parts, "dp", scatter_dimension=0, tiled=True).astype(
        jnp.float32
    )
    return (projection_output, input_cotangent, block_grads, updated_model, updated_hidden)


def solution(mesh):
    in_specs = (
        P("dp", "mp"),
        P("mp", None),
        P("mp", None, None),
        P(None, "mp"),
        P("mp", None),
        P("mp", None),
        P("dp", "mp"),
    )
    out_specs = (
        P("dp", "mp"),
        P("dp", "mp"),
        P(("mp", "dp"), None, None),
        P("mp", None),
        P("mp", None),
    )
    return jax.shard_map(shards, mesh=mesh, in_specs=in_specs, out_specs=out_specs, check_vma=False)
```
